32 devices in a mesh: dp: 4 (over x, core), ctx: 8 (over z, y).
Axes of the slice: x: 2, y: 2, z: 4, core: 2. Of those that a mesh axis runs over, the one named last changes fastest.
Arguments:
- queries: bfloat16 [16384, 32, 128], P(('dp', 'ctx')), may hold values from -8 to 8
- keys: bfloat16 [16384, 4, 128], P(('dp', 'ctx')), may hold values from -8 to 8
- values: bfloat16 [16384, 4, 128], P(('dp', 'ctx')), may hold values from -6 to 6
- doc_lengths: int32 [4, 8], P('dp'), may hold values from 1 to 1024, 4096 in all within a row
Outputs:
- attended: bfloat16 [16384, 32, 128], P(('dp', 'ctx'))
The draws below stay inside these ranges and needn't reach their ends.
All inputs are finite; a program needn't handle non-finite values.
Results may differ from the reference program's by a relative error of at most 0.0035.
Values may be sent and summed in bfloat16 or wider, within the bound.
A program may use at most 128 MiB of HBM per device.

```python
import math
import jax
import jax.numpy as jnp
import numpy as np
from jax import lax

QUERY_HEADS = 32
KEY_VALUE_HEADS = 4
HEAD_DIMENSION = 128
TILE_TOKENS = 512
SEQ = 4096
TOKEN_TOTAL = 16384
DOCS = 8
DOC_MOST = 1024
N_DP = 4
N_CTX = 8


def drawn_pair(key):
    queries = jnp.clip(jax.random.normal(jax.random.fold_in(key, 11), (TOKEN_TOTAL, QUERY_HEADS, HEAD_DIMENSION), jnp.float32), -4.0, 4.0)
    keys = jnp.clip(jax.random.normal(jax.random.fold_in(key, 12), (TOKEN_TOTAL, KEY_VALUE_HEADS, HEAD_DIMENSION), jnp.float32), -4.0, 4.0)
    return (queries, keys)


def draw_queries(key, part):
    return drawn_pair(key)[0].astype(jnp.bfloat16)


def draw_keys(key, part):
    return drawn_pair(key)[1].astype(jnp.bfloat16)


def level_of(own_key, extent, shards, least, top_value):
    gain, own = 1.0, jax.random.fold_in(own_key, 6)
    for axis_at, shards_of in shards:
        draws = jnp.exp(jax.random.uniform(jax.random.fold_in(own, axis_at), (shards_of,), jnp.float32, least / len(shards), top_value / len(shards)))
        gain = gain * jnp.repeat(draws, extent[axis_at] // shards_of).reshape([-1 if axis == axis_at else 1 for axis in range(len(extent))])
    return gain


def length_profile(count, total, most, lean):
    weights = [(1 << 20) // math.isqrt(rank ** lean) + 1 for rank in range(2, count + 1)]
    surplus, holding = total - most - (count - 1), [1] * (count - 1)
    while surplus > 0:
        free = [i for i in range(count - 1) if holding[i] < most]
        whole, remaining = sum([weights[i] for i in free]), surplus
        for i in free:
            more = min(most - holding[i], max(1, remaining * weights[i] // whole), surplus)
            holding[i] = holding[i] + more
            surplus = surplus - more
    return np.array([most] + holding)


def uneven_parts(key, amount, total, limit, slope):
    if amount == 2:
        one = jax.random.randint(key, (), max(1, total - limit), min(limit, total - 1) + 1)
        return jnp.stack([one, total - one])
    tallies = jnp.asarray(length_profile(amount, total, limit, slope), jnp.int32)
    pairs = (amount - 1) // 2
    giver, sink = tallies[1:1 + 2 * pairs:2], tallies[2:2 + 2 * pairs:2]
    room = jnp.minimum(giver - 1, limit - sink)
    moved = jax.random.randint(jax.random.fold_in(key, 1), (pairs,), 0, 1 << 20) % (room + 1)
    tallies = tallies.at[1:1 + 2 * pairs:2].set(giver - moved).at[2:2 + 2 * pairs:2].set(sink + moved)
    return tallies[jax.random.permutation(jax.random.fold_in(key, 2), amount)]


def centred(own_key, dims, scale, bound, shards=(), held_as=jnp.bfloat16):
    entries = jax.random.normal(own_key, dims, jnp.float32) * scale
    if len(shards) > 0:
        entries = level_of(own_key, dims, shards, -0.22, 0.18) * entries
    return jnp.clip(entries, min=-bound, max=bound).astype(held_as)


def setup_inputs(seed: int = 0) -> dict:
    seeds = jax.random.split(jax.random.key(seed), 5)
    queries = draw_queries(jax.random.fold_in(seeds[4], 71), 0)
    keys = draw_keys(jax.random.fold_in(seeds[4], 71), 0)
    values = centred(seeds[2], (TOKEN_TOTAL, KEY_VALUE_HEADS, HEAD_DIMENSION), 1.0, 6.0, ((0, 32),))
    doc_lengths = jax.vmap(lambda own: uneven_parts(own, DOCS, SEQ, DOC_MOST, 2))(jax.random.split(seeds[3], N_DP)).reshape((N_DP, DOCS)).astype(jnp.int32)
    return dict(queries=queries, keys=keys, values=values, doc_lengths=doc_lengths)


def doc_index(positions, lengths):
    doc_ends = jnp.cumsum(lengths)
    return lax.optimization_barrier(jnp.sum((positions[:, None] >= doc_ends[None, :]).astype(jnp.int32), axis=1))

def tile_partial(tile_queries, block_keys, block_values, query_pos, key_pos, lengths):
    tile_rows, head_count, head_width = tile_queries.shape
    kv_count = block_keys.shape[1]
    group_size = head_count // kv_count
    allowed = doc_index(query_pos, lengths)[:, None] == doc_index(key_pos, lengths)[None, :]
    allowed = allowed & (key_pos[None, :] <= query_pos[:, None]) & (key_pos[None, :] >= 0)
    score_scale = 1.0 / math.sqrt(head_width)
    grouped = tile_queries.reshape(tile_rows, kv_count, group_size, head_width).transpose(1, 0, 2, 3)
    key_heads = block_keys.transpose(1, 0, 2)
    value_heads = block_values.transpose(1, 0, 2)

    def one_head(operands):
        query_group, key_head, value_head = operands
        scores = jnp.einsum('tgd,ud->gtu', query_group.astype(jnp.float32), key_head.astype(jnp.float32)) * score_scale
        masked = jnp.where(allowed[None], scores, -1e+30)
        maxima = lax.optimization_barrier(jnp.max(masked, axis=-1))
        weights = jnp.where(allowed[None], jnp.exp(masked - maxima[..., None]), 0.0)
        sums = lax.optimization_barrier(jnp.sum(weights, axis=-1))
        rounded = weights.astype(jnp.bfloat16)
        outputs = jnp.einsum('gtu,ud->tgd', rounded.astype(jnp.float32), value_head.astype(jnp.float32))
        return (maxima, sums, outputs)
    maxima, sums, outputs = lax.map(one_head, (grouped, key_heads, value_heads))
    maxima = maxima.reshape(head_count, tile_rows)
    sums = sums.reshape(head_count, tile_rows)
    outputs = outputs.transpose(1, 0, 2, 3).reshape(tile_rows, head_count, head_width)
    return (maxima, sums, outputs)

def merge_tiles(partials):
    row_max = partials[0][0]
    for part_item in partials[1:]:
        row_max = jnp.maximum(row_max, part_item[0])
    denominator = 0.0
    weighted = 0.0
    for maxima, sums, outputs in partials:
        factor = jnp.exp(maxima - row_max)
        denominator = denominator + factor * sums
        weighted = weighted + factor.T[:, :, None] * outputs
    return (weighted / denominator.T[:, :, None]).astype(jnp.bfloat16)

def reference(queries, keys, values, doc_lengths):
    sequence_length = TILE_TOKENS * N_CTX
    key_padding = jnp.pad(keys.reshape(N_DP, sequence_length, KEY_VALUE_HEADS, HEAD_DIMENSION), ((0, 0), (2 * TILE_TOKENS, 0), (0, 0), (0, 0)))
    value_padding = jnp.pad(values.reshape(N_DP, sequence_length, KEY_VALUE_HEADS, HEAD_DIMENSION), ((0, 0), (2 * TILE_TOKENS, 0), (0, 0), (0, 0)))

    def one_tile(tile_index):
        batch_position = (tile_index // N_CTX).astype(jnp.int32)
        shard_index = (tile_index % N_CTX).astype(jnp.int32)
        tile_queries = lax.dynamic_slice_in_dim(queries, (tile_index * TILE_TOKENS).astype(jnp.int32), TILE_TOKENS, 0)
        lengths = lax.dynamic_index_in_dim(doc_lengths, batch_position, 0, False)
        query_pos = shard_index * TILE_TOKENS + jnp.arange(TILE_TOKENS, dtype=jnp.int32)
        partials = []
        for offset in (0, 1, 2):
            start_offset = ((shard_index + 2 - offset) * TILE_TOKENS).astype(jnp.int32)
            zero_value = jnp.zeros((), jnp.int32)
            block_keys = lax.dynamic_slice(key_padding, (batch_position, start_offset, zero_value, zero_value), (1, TILE_TOKENS, KEY_VALUE_HEADS, HEAD_DIMENSION))[0]
            block_values = lax.dynamic_slice(value_padding, (batch_position, start_offset, zero_value, zero_value), (1, TILE_TOKENS, KEY_VALUE_HEADS, HEAD_DIMENSION))[0]
            partials.append(tile_partial(tile_queries, block_keys, block_values, query_pos, query_pos - offset * TILE_TOKENS, lengths))
        return merge_tiles(partials)
    attended = lax.map(one_tile, jnp.arange(N_DP * N_CTX, dtype=jnp.int32))
    return attended.reshape(TOKEN_TOTAL, QUERY_HEADS, HEAD_DIMENSION)
```

```python
import functools
import math

import jax
import jax.numpy as jnp
from jax import lax
from jax.experimental import pallas as pl
from jax.experimental.pallas import tpu as pltpu
from jax.sharding import PartitionSpec as P

LANES = 128
BLOCK = 64
STRIPS = 1
MASKED = -1e30
MESH = pl.DeviceIdType.MESH


def kernel(count, lengths, q_hbm, kv_hbm, out_hbm, kbuf, qbuf, obuf, hot, bias, qsem, osem, ksem,
           far_send, far_recv, near_send, near_recv):
    heads, rows, pair = kv_hbm.shape
    width = pair // 2
    group = q_hbm.shape[1] // heads
    span = 2 * rows + LANES
    me = lax.axis_index("ctx")
    odd = lax.rem(me, 2) == 1
    partner = jnp.where(odd, me - 1, me + 1)
    has_up = me + 2 < count
    has_down = me >= 2

    barrier = pltpu.get_barrier_semaphore()

    def greet(other):
        pl.semaphore_signal(barrier, inc=1, device_id={"ctx": other}, device_id_type=MESH)

    def q_copy(h, slot):
        return pltpu.make_async_copy(
            q_hbm.at[:, pl.ds(h * group, group), :], qbuf.at[slot], qsem.at[slot]
        )

    def o_copy(h, slot):
        return pltpu.make_async_copy(
            obuf.at[slot], out_hbm.at[:, pl.ds(h * group, group), :], osem.at[slot]
        )

    def own_copy(h):
        return pltpu.make_async_copy(
            kv_hbm.at[h], kbuf.at[h, pl.ds(2 * rows, rows), :], ksem.at[h]
        )

    def far_copy(h):
        return pltpu.make_async_remote_copy(
            src_ref=kv_hbm.at[h],
            dst_ref=kbuf.at[h, pl.ds(0, rows), :],
            send_sem=far_send.at[h],
            recv_sem=far_recv.at[h],
            device_id={"ctx": me + 2},
            device_id_type=MESH,
        )

    def near_own_copy(h):
        return pltpu.make_async_remote_copy(
            src_ref=kv_hbm.at[h],
            dst_ref=kbuf.at[h, pl.ds(rows, rows), :],
            send_sem=near_send.at[h],
            recv_sem=near_recv.at[h],
            device_id={"ctx": partner},
            device_id_type=MESH,
        )

    def near_relay_copy(h):
        return pltpu.make_async_remote_copy(
            src_ref=kbuf.at[h, pl.ds(0, rows), :],
            dst_ref=kbuf.at[h, pl.ds(rows, rows), :],
            send_sem=near_send.at[h],
            recv_sem=near_recv.at[h],
            device_id={"ctx": partner},
            device_id_type=MESH,
        )

    greet(partner)

    @pl.when(has_up)
    def _():
        greet(me + 2)

    @pl.when(has_down)
    def _():
        greet(me - 2)

    q_copy(0, 0).start()
    for h in range(heads):
        own_copy(h).start()

    pl.semaphore_wait(barrier, 1 + has_up.astype(jnp.int32) + has_down.astype(jnp.int32))

    @pl.when(has_up)
    def _():
        for h in range(heads):
            far_copy(h).start()

    @pl.when(jnp.logical_not(odd))
    def _():
        for h in range(heads):
            near_own_copy(h).start()

    @pl.when(me < 2)
    def _():
        kbuf[:, 0:rows, :] = jnp.zeros((heads, rows, pair), kbuf.dtype)

    @pl.when(me < 1)
    def _():
        kbuf[:, rows : 2 * rows, :] = jnp.zeros((heads, rows, pair), kbuf.dtype)

    row_token = lax.broadcasted_iota(jnp.int32, (BLOCK, group, LANES), 0)
    lane = lax.broadcasted_iota(jnp.int32, (BLOCK, group, LANES), 2)
    hot[...] = (
        jnp.where(row_token == lane, 1.0, 0.0).reshape(BLOCK * group, LANES).astype(hot.dtype)
    )

    def window_of(block):
        return ((block * BLOCK) // LANES) * LANES

    def fill_bias(block, carry):
        base = me * rows
        token = base + block * BLOCK + lax.broadcasted_iota(jnp.int32, (1, LANES), 1)
        first = jnp.zeros((1, LANES), jnp.int32)
        end = jnp.int32(0)
        for d in range(lengths.shape[1]):
            end = end + lengths[0, d]
            first = jnp.where(token >= end, end, first)
        key = base - 2 * rows + window_of(block) + lax.broadcasted_iota(jnp.int32, (span, LANES), 0)
        allowed = (key >= first) & (key <= token)
        bias[block] = jnp.where(allowed, 0.0, MASKED).astype(bias.dtype)
        return carry

    lax.fori_loop(0, rows // BLOCK, fill_bias, 0)

    factor = math.log2(math.e) / math.sqrt(width)
    ones = jnp.ones((span, LANES), kbuf.dtype)

    def one_head(h, carry):
        slot = lax.rem(h, 2)
        q_copy(h, slot).wait()

        @pl.when(h + 1 < heads)
        def _():
            q_copy(h + 1, 1 - slot).start()

        own_copy(h).wait()

        @pl.when(has_down)
        def _():
            far_copy(h).wait_recv()

        @pl.when(has_down & odd)
        def _():
            near_relay_copy(h).start()

        @pl.when(me >= 1)
        def _():
            near_own_copy(h).wait_recv()

        @pl.when(h >= 2)
        def _():
            o_copy(h - 2, slot).wait()

        def one_block(block, inner):
            window = pl.ds(pl.multiple_of(window_of(block), LANES), span)
            both = kbuf[h, window, :]
            keys = jnp.concatenate([both[:, :width], bias[block]], axis=1)
            values = jnp.concatenate([both[:, width:], ones], axis=1)
            tokens = BLOCK // STRIPS
            for s in range(STRIPS):
                at = pl.ds(pl.multiple_of(block * BLOCK, BLOCK) + s * tokens, tokens)
                q = qbuf[slot, at].reshape(tokens * group, width)
                q = jnp.concatenate([q, hot[s * tokens * group : (s + 1) * tokens * group]], axis=1)
                scores = lax.dot_general(
                    q, keys, (((1,), (1,)), ((), ())), preferred_element_type=jnp.float32
                )
                top = jnp.max(scores, axis=1, keepdims=True)
                weights = jnp.exp2((scores - top) * factor).astype(kbuf.dtype)
                total = jnp.dot(weights, values, preferred_element_type=jnp.float32)
                result = total[:, :width] / total[:, width : 2 * width]
                obuf[slot, at] = result.reshape(tokens, group, width).astype(obuf.dtype)
            return inner

        lax.fori_loop(0, rows // BLOCK, one_block, 0)
        o_copy(h, slot).start()
        return carry

    lax.fori_loop(0, heads, one_head, 0)

    for h in range(max(0, heads - 2), heads):
        o_copy(h, h % 2).wait()

    @pl.when(has_up)
    def _():
        for h in range(heads):
            far_copy(h).wait_send()

    @pl.when(jnp.logical_not(odd))
    def _():
        for h in range(heads):
            near_own_copy(h).wait_send()

    @pl.when(has_down & odd)
    def _():
        for h in range(heads):
            near_relay_copy(h).wait_send()


def body(count, queries, keys, values, doc_lengths):
    rows, query_heads, width = queries.shape
    heads = keys.shape[1]
    group = query_heads // heads
    key_value = jnp.concatenate([keys, values], axis=-1).transpose(1, 0, 2)
    blocks = rows // BLOCK
    span = 2 * rows + LANES
    any_space = pl.BlockSpec(memory_space=pl.ANY)
    return pl.pallas_call(
        functools.partial(kernel, count),
        out_shape=jax.ShapeDtypeStruct(queries.shape, queries.dtype),
        in_specs=[pl.BlockSpec(memory_space=pltpu.SMEM), any_space, any_space],
        out_specs=any_space,
        scratch_shapes=[
            pltpu.VMEM((heads, 3 * rows, 2 * width), keys.dtype),
            pltpu.VMEM((2, rows, group, width), queries.dtype),
            pltpu.VMEM((2, rows, group, width), queries.dtype),
            pltpu.VMEM((BLOCK * group, LANES), queries.dtype),
            pltpu.VMEM((blocks, span, LANES), queries.dtype),
            pltpu.SemaphoreType.DMA((2,)),
            pltpu.SemaphoreType.DMA((2,)),
            pltpu.SemaphoreType.DMA((heads,)),
            pltpu.SemaphoreType.DMA((heads,)),
            pltpu.SemaphoreType.DMA((heads,)),
            pltpu.SemaphoreType.DMA((heads,)),
            pltpu.SemaphoreType.DMA((heads,)),
        ],
        compiler_params=pltpu.CompilerParams(
            collective_id=0, has_side_effects=True, vmem_limit_bytes=56 * 1024 * 1024
        ),
    )(doc_lengths, queries, key_value)


def solution(mesh):
    placed = (
        P(("dp", "ctx"), None, None),
        P(("dp", "ctx"), None, None),
        P(("dp", "ctx"), None, None),
        P("dp", None),
    )
    return jax.shard_map(
        functools.partial(body, mesh.shape["ctx"]),
        mesh=mesh,
        in_specs=placed,
        out_specs=P(("dp", "ctx"), None, None),
        check_vma=False,
    )
```

```python
import functools
import math

import jax
import jax.numpy as jnp
from jax import lax
from jax.experimental import pallas as pl
from jax.experimental.pallas import tpu as pltpu
from jax.sharding import PartitionSpec as P

LANES = 128
BLOCK = 64
MASKED = -1e30
MESH = pl.DeviceIdType.MESH


def kernel(count, lengths, q_hbm, k_hbm, v_hbm, out_hbm, kbuf, vbuf, qbuf, obuf, hot, bias, scores_a,
           scores_b, tops_a, tops_b, qsem, osem, ksem, far_send, far_recv, near_send, near_recv):
    heads, rows, width = k_hbm.shape
    parts = ((k_hbm, kbuf), (v_hbm, vbuf))
    group = q_hbm.shape[1] // heads
    span = 2 * rows + LANES
    me = lax.axis_index("ctx")
    odd = lax.rem(me, 2) == 1
    partner = jnp.where(odd, me - 1, me + 1)
    has_up = me + 2 < count
    has_down = me >= 2

    barrier = pltpu.get_barrier_semaphore()

    def greet(other):
        pl.semaphore_signal(barrier, inc=1, device_id={"ctx": other}, device_id_type=MESH)

    def q_copy(h, slot):
        return pltpu.make_async_copy(
            q_hbm.at[:, pl.ds(h * group, group), :], qbuf.at[slot], qsem.at[slot]
        )

    def o_copy(h, slot):
        return pltpu.make_async_copy(
            obuf.at[slot], out_hbm.at[:, pl.ds(h * group, group), :], osem.at[slot]
        )

    def own_copy(h, part):
        source, held = parts[part]
        return pltpu.make_async_copy(
            source.at[h], held.at[h, pl.ds(2 * rows, rows), :], ksem.at[2 * h + part]
        )

    def far_copy(h, part):
        source, held = parts[part]
        return pltpu.make_async_remote_copy(
            src_ref=source.at[h],
            dst_ref=held.at[h, pl.ds(0, rows), :],
            send_sem=far_send.at[2 * h + part],
            recv_sem=far_recv.at[2 * h + part],
            device_id={"ctx": me + 2},
            device_id_type=MESH,
        )

    def near_own_copy(h, part):
        source, held = parts[part]
        return pltpu.make_async_remote_copy(
            src_ref=source.at[h],
            dst_ref=held.at[h, pl.ds(rows, rows), :],
            send_sem=near_send.at[2 * h + part],
            recv_sem=near_recv.at[2 * h + part],
            device_id={"ctx": partner},
            device_id_type=MESH,
        )

    def near_relay_copy(h, part):
        held = parts[part][1]
        return pltpu.make_async_remote_copy(
            src_ref=held.at[h, pl.ds(0, rows), :],
            dst_ref=held.at[h, pl.ds(rows, rows), :],
            send_sem=near_send.at[2 * h + part],
            recv_sem=near_recv.at[2 * h + part],
            device_id={"ctx": partner},
            device_id_type=MESH,
        )

    greet(partner)

    @pl.when(has_up)
    def _():
        greet(me + 2)

    @pl.when(has_down)
    def _():
        greet(me - 2)

    q_copy(0, 0).start()
    for h in range(heads):
        for part in range(2):
            own_copy(h, part).start()

    pl.semaphore_wait(barrier, 1 + has_up.astype(jnp.int32) + has_down.astype(jnp.int32))

    @pl.when(has_up)
    def _():
        for h in range(heads):
            for part in range(2):
                far_copy(h, part).start()

    @pl.when(jnp.logical_not(odd))
    def _():
        for h in range(heads):
            for part in range(2):
                near_own_copy(h, part).start()

    @pl.when(me < 2)
    def _():
        for held in (kbuf, vbuf):
            held[:, 0:rows, :] = jnp.zeros((heads, rows, width), held.dtype)

    @pl.when(me < 1)
    def _():
        for held in (kbuf, vbuf):
            held[:, rows : 2 * rows, :] = jnp.zeros((heads, rows, width), held.dtype)

    row_token = lax.broadcasted_iota(jnp.int32, (BLOCK, group, LANES), 0)
    lane = lax.broadcasted_iota(jnp.int32, (BLOCK, group, LANES), 2)
    hot[...] = (
        jnp.where(row_token == lane, 1.0, 0.0).reshape(BLOCK * group, LANES).astype(hot.dtype)
    )

    def window_of(block):
        return ((block * BLOCK) // LANES) * LANES

    def fill_bias(block, carry):
        base = me * rows
        token = base + block * BLOCK + lax.broadcasted_iota(jnp.int32, (1, LANES), 1)
        first = jnp.zeros((1, LANES), jnp.int32)
        end = jnp.int32(0)
        for d in range(lengths.shape[1]):
            end = end + lengths[0, d]
            first = jnp.where(token >= end, end, first)
        key = base - 2 * rows + window_of(block) + lax.broadcasted_iota(jnp.int32, (span, LANES), 0)
        allowed = (key >= first) & (key <= token)
        bias[block] = jnp.where(allowed, 0.0, MASKED).astype(bias.dtype)
        return carry

    lax.fori_loop(0, rows // BLOCK, fill_bias, 0)

    factor = math.log2(math.e) / math.sqrt(width)
    ones = jnp.ones((span, LANES), kbuf.dtype)

    blocks = rows // BLOCK
    steps = heads * blocks

    def advance(h):
        @pl.when(has_down)
        def _():
            for part in range(2):
                far_copy(h, part).wait_recv()

                @pl.when(odd)
                def _():
                    near_relay_copy(h, part).start()

    def open_head(h):
        q_copy(h, lax.rem(h, 2)).wait()
        for part in range(2):
            own_copy(h, part).wait()

        @pl.when(me >= 1)
        def _():
            for part in range(2):
                near_own_copy(h, part).wait_recv()

    def score_stage(step, scores, tops):
        h, block = step // blocks, lax.rem(step, blocks)
        window = pl.ds(pl.multiple_of(window_of(block), LANES), span)
        keys = jnp.concatenate([kbuf[h, window, :], bias[block]], axis=1)
        at = pl.ds(pl.multiple_of(block * BLOCK, BLOCK), BLOCK)
        q = qbuf[lax.rem(h, 2), at].reshape(BLOCK * group, width)
        q = jnp.concatenate([q, hot[...]], axis=1)
        found = lax.dot_general(
            q, keys, (((1,), (1,)), ((), ())), preferred_element_type=jnp.float32
        )
        scores[...] = found
        tops[...] = jnp.broadcast_to(jnp.max(found, axis=1, keepdims=True), tops.shape)

    def value_stage(step, scores, tops):
        h, block = step // blocks, lax.rem(step, blocks)
        window = pl.ds(pl.multiple_of(window_of(block), LANES), span)
        values = jnp.concatenate([vbuf[h, window, :], ones], axis=1)
        at = pl.ds(pl.multiple_of(block * BLOCK, BLOCK), BLOCK)
        top = jnp.concatenate([tops[...]] * (span // LANES), axis=1)
        weights = jnp.exp2((scores[...] - top) * factor).astype(kbuf.dtype)
        total = jnp.dot(weights, values, preferred_element_type=jnp.float32)
        result = total[:, :width] / total[:, width : 2 * width]
        obuf[lax.rem(h, 2), at] = result.reshape(BLOCK, group, width).astype(obuf.dtype)

    advance(0)
    open_head(0)
    score_stage(0, scores_a, tops_a)

    def two_steps(pair_index, carry):
        step = pair_index * 2
        h, block = step // blocks, lax.rem(step, blocks)

        @pl.when((block == 0) & (h >= 2))
        def _():
            o_copy(h - 2, lax.rem(h, 2)).wait()

        @pl.when((block == 0) & (h + 1 < heads))
        def _():
            q_copy(h + 1, lax.rem(h + 1, 2)).start()

        @pl.when((block == ((blocks // 2) // 2) * 2) & (h + 1 < heads))
        def _():
            advance(h + 1)

        @pl.when((block == blocks - 2) & (h + 1 < heads))
        def _():
            open_head(h + 1)

        score_stage(step + 1, scores_b, tops_b)
        value_stage(step, scores_a, tops_a)
        score_stage(jnp.minimum(step + 2, steps - 1), scores_a, tops_a)
        value_stage(step + 1, scores_b, tops_b)

        @pl.when(block == blocks - 2)
        def _():
            o_copy(h, lax.rem(h, 2)).start()

        return carry

    lax.fori_loop(0, steps // 2, two_steps, 0)

    for h in range(max(0, heads - 2), heads):
        o_copy(h, h % 2).wait()

    @pl.when(has_up)
    def _():
        for h in range(heads):
            for part in range(2):
                far_copy(h, part).wait_send()

    @pl.when(jnp.logical_not(odd))
    def _():
        for h in range(heads):
            for part in range(2):
                near_own_copy(h, part).wait_send()

    @pl.when(has_down & odd)
    def _():
        for h in range(heads):
            for part in range(2):
                near_relay_copy(h, part).wait_send()


def body(count, queries, keys, values, doc_lengths):
    rows, query_heads, width = queries.shape
    heads = keys.shape[1]
    group = query_heads // heads
    blocks = rows // BLOCK
    span = 2 * rows + LANES
    any_space = pl.BlockSpec(memory_space=pl.ANY)
    return pl.pallas_call(
        functools.partial(kernel, count),
        out_shape=jax.ShapeDtypeStruct(queries.shape, queries.dtype),
        in_specs=[pl.BlockSpec(memory_space=pltpu.SMEM), any_space, any_space, any_space],
        out_specs=any_space,
        scratch_shapes=[
            pltpu.VMEM((heads, 3 * rows, width), keys.dtype),
            pltpu.VMEM((heads, 3 * rows, width), keys.dtype),
            pltpu.VMEM((2, rows, group, width), queries.dtype),
            pltpu.VMEM((2, rows, group, width), queries.dtype),
            pltpu.VMEM((BLOCK * group, LANES), queries.dtype),
            pltpu.VMEM((blocks, span, LANES), queries.dtype),
            pltpu.VMEM((BLOCK * group, span), jnp.float32),
            pltpu.VMEM((BLOCK * group, span), jnp.float32),
            pltpu.VMEM((BLOCK * group, LANES), jnp.float32),
            pltpu.VMEM((BLOCK * group, LANES), jnp.float32),
            pltpu.SemaphoreType.DMA((2,)),
            pltpu.SemaphoreType.DMA((2,)),
            pltpu.SemaphoreType.DMA((2 * heads,)),
            pltpu.SemaphoreType.DMA((2 * heads,)),
            pltpu.SemaphoreType.DMA((2 * heads,)),
            pltpu.SemaphoreType.DMA((2 * heads,)),
            pltpu.SemaphoreType.DMA((2 * heads,)),
        ],
        compiler_params=pltpu.CompilerParams(
            collective_id=0, has_side_effects=True, vmem_limit_bytes=56 * 1024 * 1024
        ),
    )(doc_lengths, queries, keys.transpose(1, 0, 2), values.transpose(1, 0, 2))


def solution(mesh):
    placed = (
        P(("dp", "ctx"), None, None),
        P(("dp", "ctx"), None, None),
        P(("dp", "ctx"), None, None),
        P("dp", None),
    )
    return jax.shard_map(
        functools.partial(body, mesh.shape["ctx"]),
        mesh=mesh,
        in_specs=placed,
        out_specs=P(("dp", "ctx"), None, None),
        check_vma=False,
    )
```
